32 devices in a mesh: region: 8 (over y, x, core), member: 4 (over z).
Axes of the slice: x: 2, y: 2, z: 4, core: 2. Of those that a mesh axis runs over, the one named last changes fastest.
Arguments:
- prior_states: float32 [16, 256, 4, 2048], P('region', 'member'), may hold values from -6 to 6
- prior_in_sensor_space: float32 [16, 256, 256], P('region', 'member'), may hold values from -10 to 10
- sensor_readings: float32 [16, 256], replicated, may hold values from -8 to 8
- error_precisions: float32 [16, 256], replicated, may hold values from 0.25 to 4
- live_tallies: int32 [16], replicated, may hold values from 1 to 256
- adjacent_areas: int32 [16, 4], replicated, may hold values from 0 to 15, as said below
- taper_lookup: int32 [16, 5, 256], replicated, may hold values from 0 to 15
- blend_lookup: int32 [16, 4, 5], P('region', 'member'), may hold values from 0 to 15
- taper_factors: float32 [16], replicated, may hold values from 0.05 to 1
Outputs:
- analysis: float32 [16, 256, 4, 2048], P('region', 'member')
The draws below stay inside these ranges and needn't reach their ends.
Inputs may be any that keep to these rules, and one draw needn't show every extreme that they name: `adjacent_areas`: the 4 neighbours of region r are distinct, differ from r, and each neighbour q satisfies (q // 2 - r // 2) equal to -1, 0 or 1 modulo 16 // 2.
All inputs are finite; a program needn't handle non-finite values.
Results may differ from the reference program's by a relative error of at most 0.0003.
Values sent between devices are 32-bit elements; how exact they have to be, the bound alone decides.
A program may use at most 64 MiB of HBM per device.

```python
import math
import jax
import jax.numpy as jnp
from jax import lax

MEMBER_TOTAL = 256
NOBS = 256
NBR = 4
LEVELS = 16
NSIT = 8
REG_DEV = 2
TILE_POINTS = 2048
AREA_TOTAL = 16
TILES_PER_AREA = 4


def draw_adjacent_areas(key, part):
    slot_count = 3 * REG_DEV
    dev_count = AREA_TOTAL // REG_DEV
    area_batch = jnp.arange(AREA_TOTAL, dtype=jnp.int32)
    own_slot = REG_DEV + area_batch % REG_DEV
    slot_ids = jnp.arange(slot_count, dtype=jnp.int32)
    scores = jax.random.randint(jax.random.fold_in(key, 11), (AREA_TOTAL, slot_count), 0, 1 << 20, dtype=jnp.int32) * slot_count + slot_ids[None, :]
    scores = jnp.where(slot_ids[None, :] == own_slot[:, None], 1 << 30, scores)
    chosen = jnp.argsort(scores, axis=1, stable=True)[:, :NBR].astype(jnp.int32)
    device = area_batch // REG_DEV
    target = (device[:, None] + chosen // REG_DEV - 1) % dev_count * REG_DEV + chosen % REG_DEV
    return target.astype(jnp.int32)


def draw_prior_in_sensor_space(key, part):
    noise_key = jax.random.fold_in(key, 21)
    member_key = jax.random.fold_in(key, 22)
    column_key = jax.random.fold_in(key, 23)
    column_mode = jnp.clip(jax.random.normal(column_key, (AREA_TOTAL, NOBS), jnp.float32), -3.0, 3.0)
    noise = jnp.clip(jax.random.normal(noise_key, (AREA_TOTAL, MEMBER_TOTAL, NOBS), jnp.float32), -4.0, 4.0)
    member_mode = jnp.clip(jax.random.normal(member_key, (MEMBER_TOTAL,), jnp.float32), -3.0, 3.0)
    strength = 0.8
    values = noise + strength * member_mode[None, :, None] * column_mode[:, None, :]
    return jnp.clip(values, -10.0, 10.0).astype(jnp.float32)


def plant(result, own_key, low, top_value):
    spot = [jax.random.randint(jax.random.fold_in(own_key, axis), (), 0, length) for axis, length in enumerate(result.shape)]
    widest = result.shape.index(max(result.shape))
    neighbour = spot[:widest] + [(spot[widest] + 1) % result.shape[widest]] + spot[widest + 1:]
    return result.at[tuple(spot)].set(low).at[tuple(neighbour)].set(top_value)


def block_scale(stream_key, dims, pieces, least, largest):
    def one(dim, parts):
        heights = jax.random.uniform(jax.random.fold_in(jax.random.fold_in(stream_key, 6), dim), (parts,), jnp.float32, least / len(pieces), largest / len(pieces))
        return jnp.repeat(jnp.exp(heights), dims[dim] // parts).reshape((-1,) + (1,) * (len(dims) - dim - 1))

    gain = one(*pieces[0])
    for cut in pieces[1:]:
        gain = gain * one(*cut)
    return gain


def bell_draw(rng, shape, deviation, most, cuts=(), kind=jnp.bfloat16):
    drawn = jax.random.normal(rng, shape, jnp.float32) * deviation
    if len(cuts) > 0:
        drawn = block_scale(rng, shape, cuts, -0.22, 0.18) * drawn
    return jnp.clip(drawn, min=-most, max=most).astype(kind)


def setup_inputs(seed: int = 0) -> dict:
    key_of = jax.random.split(jax.random.key(seed), 10)
    return {
        "prior_states": bell_draw(key_of[0], (AREA_TOTAL, MEMBER_TOTAL, TILES_PER_AREA, TILE_POINTS), 1.0, 6.0, ((0, 8), (1, 4)), jnp.float32),
        "prior_in_sensor_space": draw_prior_in_sensor_space(jax.random.fold_in(key_of[9], 71), 0),
        "sensor_readings": bell_draw(key_of[2], (AREA_TOTAL, NOBS), 1.5, 8.0, (), jnp.float32),
        "error_precisions": jnp.clip(jnp.exp(jax.random.uniform(key_of[3], (AREA_TOTAL, NOBS), jnp.float32, math.log(0.25), math.log(4.0))), 0.25, 4.0),
        "live_tallies": plant(jax.random.randint(key_of[4], (AREA_TOTAL,), 1, NOBS + 1), jax.random.fold_in(key_of[4], 1), 1, NOBS).astype(jnp.int32),
        "adjacent_areas": draw_adjacent_areas(jax.random.fold_in(key_of[9], 71), 0),
        "taper_lookup": plant(jax.random.randint(key_of[6], (AREA_TOTAL, NBR + 1, NOBS), 0, LEVELS), jax.random.fold_in(key_of[6], 1), 0, LEVELS - 1).astype(jnp.int32),
        "blend_lookup": plant(jax.random.randint(key_of[7], (AREA_TOTAL, TILES_PER_AREA, NBR + 1), 0, LEVELS), jax.random.fold_in(key_of[7], 1), 0, LEVELS - 1).astype(jnp.int32),
        "taper_factors": jnp.clip(jnp.exp(jax.random.uniform(key_of[8], (LEVELS,), jnp.float32, math.log(0.05), math.log(1.0))), 0.05, 1.0),
    }


inflation = 1.1
highest = lax.Precision.HIGHEST

def newton_root(gram_mat):
    order = gram_mat.shape[-1]
    identity = jnp.eye(order, dtype=jnp.float32)
    norm_value = jnp.sqrt(lax.optimization_barrier(jnp.sum(gram_mat * gram_mat, axis=(-2, -1))))
    scaled = gram_mat / norm_value[..., None, None]
    root_mat = jnp.broadcast_to(identity, gram_mat.shape)
    for sweep in range(NSIT):
        correction = 1.5 * identity - 0.5 * jnp.einsum('...ij,...jk->...ik', root_mat, scaled, precision=highest)
        root_mat = jnp.einsum('...ij,...jk->...ik', correction, root_mat, precision=highest)
        if sweep + 1 < NSIT:
            scaled = jnp.einsum('...ij,...jk->...ik', scaled, correction, precision=highest)
    return (root_mat, norm_value)

def transform_of(gram_mat, drive_vec):
    members = gram_mat.shape[-1]
    root_mat, norm_value = newton_root(gram_mat)
    half_way = jnp.einsum('...jk,...k->...j', root_mat, drive_vec, precision=highest)
    mean_shift = jnp.einsum('...jk,...k->...j', root_mat, half_way, precision=highest) / norm_value[..., None]
    factor = jnp.sqrt(members - 1.0) / jnp.sqrt(norm_value)
    return factor[..., None, None] * root_mat + mean_shift[..., None]

def reference(prior_states, prior_in_sensor_space, sensor_readings, error_precisions, live_tallies, adjacent_areas, taper_lookup, blend_lookup, taper_factors):
    ens_mean = lax.optimization_barrier(jnp.mean(prior_in_sensor_space, axis=1))
    perturb = prior_in_sensor_space - ens_mean[:, None, :]
    live_mask = (jnp.arange(NOBS, dtype=jnp.int32)[None, :] < live_tallies[:, None]).astype(jnp.float32)
    obs_weight = error_precisions * live_mask
    innovation = sensor_readings - ens_mean
    blocks = jnp.concatenate([jnp.arange(AREA_TOTAL, dtype=jnp.int32)[:, None], adjacent_areas.astype(jnp.int32)], axis=1).astype(jnp.int32)
    local_weight = jnp.take(taper_factors, taper_lookup, axis=0)
    identity = jnp.eye(MEMBER_TOTAL, dtype=jnp.float32)

    def one_region(area_batch):
        chosen = blocks[area_batch]
        pert_sel = jnp.take(perturb, chosen, axis=0)
        weight_sel = jnp.take(obs_weight, chosen, axis=0) * local_weight[area_batch]
        innov_sel = jnp.take(innovation, chosen, axis=0)
        weighted = pert_sel * weight_sel[:, None, :]
        gram_mat = jnp.einsum('bkm,bjm->kj', weighted, pert_sel, precision=highest) + (MEMBER_TOTAL - 1) / inflation * identity
        drive_vec = jnp.einsum('bkm,bm->k', weighted, innov_sel, precision=highest)
        return transform_of(gram_mat, drive_vec)
    transforms = lax.map(one_region, jnp.arange(AREA_TOTAL, dtype=jnp.int32))
    blend_weight = jnp.take(taper_factors, blend_lookup, axis=0)
    blend_weight = blend_weight / lax.optimization_barrier(jnp.sum(blend_weight, axis=-1, keepdims=True))

    def update_region(area_batch):
        picked = jnp.take(transforms, blocks[area_batch], axis=0)
        patch_transform = jnp.einsum('qb,bjk->qjk', blend_weight[area_batch], picked, precision=highest)
        area_sorted = prior_states[area_batch]
        center = lax.optimization_barrier(jnp.mean(area_sorted, axis=0, keepdims=True))
        return center + jnp.einsum('qjk,jqv->kqv', patch_transform, area_sorted - center, precision=highest)
    return lax.map(update_region, jnp.arange(AREA_TOTAL, dtype=jnp.int32))
```

```python
import functools
import jax
import jax.numpy as jnp
from jax import lax
from jax.experimental import pallas as pl
from jax.experimental.pallas import tpu as pltpu
from jax.sharding import PartitionSpec as P

NSIT = 8
LANES = 128
inflation = 1.1
highest = lax.Precision.HIGHEST
MESH = pl.DeviceIdType.MESH


def mm(a, b, dims=(((1,), (0,)), ((), ()))):
    return lax.dot_general(a, b, dims, precision=highest, preferred_element_type=jnp.float32)


def kernel(
    n,
    ring,
    hx_ref,
    read_hbm,
    prec_hbm,
    look_hbm,
    live_hbm,
    adj_hbm,
    blend_hbm,
    taper_hbm,
    x_ref,
    out_ref,
    read_ref,
    prec_ref,
    look_ref,
    live_ref,
    adj_ref,
    blend_ref,
    taper_ref,
    xs,
    ob,
    hxb,
    tb,
    scaled,
    root,
    drive,
    ptt,
    x_send,
    x_recv,
    x_local,
    o_send,
    o_recv,
    o_local,
    h_up,
    h_down,
    h_recv,
    h_local,
    small,
    n_send,
    n_recv,
    t_send,
    t_recv,
    met,
):
    me = lax.axis_index("member")
    pos = lax.axis_index("region")
    here = x_ref.shape[0]
    block = x_ref.shape[1]
    cols = x_ref.shape[2]
    members = n * block
    nobs = hx_ref.shape[2]
    blocks = look_ref.shape[0]
    left, right = lax.rem(pos + ring - 1, ring), lax.rem(pos + 1, ring)
    half = n // 2
    low = me < half
    inner = jnp.where(low, me + 1, me - 1)
    outer = jnp.where(low, me - 1, me + 1)
    middle = (me == half - 1) | (me == half)
    edge = (me == 0) | (me == n - 1)

    def partner(i):
        up = n - 1 - i
        return jnp.where(low, jnp.where(up <= me, up - 1, up), jnp.where(i >= me, i + 1, i))

    def far(i):
        up = n - 1 - i
        return jnp.where(low, jnp.where(up < me + 2, up - 2, up), jnp.where(i < me - 1, i, i + 2))

    def tell(sem, **where):
        pl.semaphore_signal(sem, inc=1, device_id=where, device_id_type=MESH)

    barrier = pltpu.get_barrier_semaphore()

    @pl.when(middle)
    def _():
        tell(barrier, member=inner)

    @pl.when(jnp.logical_not(edge))
    def _():
        tell(barrier, member=outer)
        pl.semaphore_wait(barrier, 1)

    @pl.when(edge)
    def _():
        for side in (left, right):
            tell(barrier, region=side)
        pl.semaphore_wait(barrier, 3)

    def rows(who):
        return pl.ds(pl.multiple_of(who * block, block), block)

    def h_copy(owner, up, own=False):
        kept = hxb.at[pl.ds(here, here), rows(owner)]
        return pltpu.make_async_remote_copy(
            hx_ref if own else kept,
            kept,
            (h_up if up else h_down).at[owner],
            h_recv.at[owner],
            device_id={"member": me + 1 if up else me - 1},
            device_id_type=MESH,
        )

    def h_send(owner, up, act, own=False):
        @pl.when(me < n - 1 if up else me > 0)
        def _():
            getattr(h_copy(owner, up, own), act)()

    def x_copy(r, peer, owner):
        return pltpu.make_async_remote_copy(
            x_ref.at[r, :, :, peer, :],
            xs.at[r, rows(owner)],
            x_send.at[r, peer],
            x_recv.at[r, owner],
            device_id={"member": peer},
            device_id_type=MESH,
        )

    def o_copy(r, peer, owner):
        return pltpu.make_async_remote_copy(
            ob.at[r, rows(peer)],
            out_ref.at[r, :, :, owner, :],
            o_send.at[r, peer],
            o_recv.at[r, owner],
            device_id={"member": peer},
            device_id_type=MESH,
        )

    def beside(buf, send, recv, part=None, src=None):
        def at(slot):
            where = buf.at[pl.ds(slot * here, here)]
            return where if part is None else where.at[:, rows(part)]

        def sems(ref, side):
            return ref.at[side] if part is None else ref.at[side, part]

        mine = at(1) if src is None else src
        return (
            pltpu.make_async_remote_copy(
                mine,
                at(2),
                sems(send, 0),
                sems(recv, 0),
                device_id={"region": left},
                device_id_type=MESH,
            ),
            pltpu.make_async_remote_copy(
                mine,
                at(0),
                sems(send, 1),
                sems(recv, 1),
                device_id={"region": right},
                device_id_type=MESH,
            ),
        )

    def h_beside(owner, src=None):
        return beside(hxb, n_send, n_recv, owner, src)

    own_h = pltpu.make_async_copy(hx_ref, hxb.at[pl.ds(here, here), rows(me)], h_local)
    tables = (
        (read_hbm, read_ref),
        (prec_hbm, prec_ref),
        (look_hbm, look_ref),
        (live_hbm, live_ref),
        (adj_hbm, adj_ref),
        (blend_hbm, blend_ref),
        (taper_hbm, taper_ref),
    )
    fetches = [pltpu.make_async_copy(*t, small.at[i]) for i, t in enumerate(tables)]
    own_x = [
        pltpu.make_async_copy(x_ref.at[r, :, :, me, :], xs.at[r, rows(me)], x_local.at[r])
        for r in range(here)
    ]
    @pl.when(low)
    def _():
        h_copy(me, True, True).start()

    @pl.when(jnp.logical_not(low))
    def _():
        h_copy(me, False, True).start()

    @pl.when(middle)
    def _():
        x_copy(0, inner, me).start()

    @pl.when(jnp.logical_not(edge))
    def _():
        pl.semaphore_wait(met.at[0], 1)

    @pl.when(jnp.logical_not(middle))
    def _():
        tell(met.at[0], member=inner)

    @pl.when(middle)
    def _():
        tell(met.at[1], member=inner)

    pl.semaphore_wait(met.at[1], 1)

    @pl.when(jnp.logical_not(edge))
    def _():
        tell(met.at[1], member=outer)

    @pl.when(low & jnp.logical_not(edge))
    def _():
        h_copy(me, False, True).start()

    @pl.when(jnp.logical_not(low | edge))
    def _():
        h_copy(me, True, True).start()

    @pl.when(jnp.logical_not(middle))
    def _():
        x_copy(0, partner(0), me).start()

    @pl.when(edge)
    def _():
        tell(met.at[2], region=right)
        tell(met.at[3], region=left)
        pl.semaphore_wait(met.at[2], 1)
        pl.semaphore_wait(met.at[3], 1)

        @pl.when(jnp.logical_not(middle))
        def _():
            tell(met.at[4], member=inner)

    for copy in [own_h] + fetches:
        copy.start()

    @pl.when(jnp.logical_not(edge))
    def _():
        pl.semaphore_wait(met.at[4], 1)

        @pl.when(jnp.logical_not(middle))
        def _():
            tell(met.at[4], member=inner)

    for copy in h_beside(me, hx_ref):
        copy.start()
    for s in range(1, n):
        @pl.when(me - s >= 0)
        def _():
            h_copy(me - s, True).wait_recv()
            h_send(me - s, True, "start")
            for copy in h_beside(me - s):
                copy.start()

        @pl.when(me + s < n)
        def _():
            h_copy(me + s, False).wait_recv()
            h_send(me + s, False, "start")
            for copy in h_beside(me + s):
                copy.start()

        if s == 1:
            for i in range(n - 2):
                x_copy(0, jnp.where(middle, far(i), partner(i + 1)), me).start()
    for r in range(1, here):
        for i in range(n - 1):
            x_copy(r, partner(i), me).start()
    for copy in own_x:
        copy.start()
    for copy in [own_h] + fetches:
        copy.wait()
    for owner in range(n):
        for copy in h_beside(owner):
            copy.wait()

    lane = lax.broadcasted_iota(jnp.int32, (1, nobs), 1)
    line = lax.broadcasted_iota(jnp.int32, (members, members), 0)
    cross = lax.broadcasted_iota(jnp.int32, (members, members), 1)
    eye = jnp.where(line == cross, 1.0, 0.0).astype(jnp.float32)
    norms = []

    def area_of(r, b):
        mine = pos * here + r
        return mine if b == 0 else adj_ref[b - 1, mine]

    def slot_of(area):
        slot = lax.rem(area // here - pos + 1 + ring, ring) * here + lax.rem(area, here)
        return jnp.minimum(slot, 3 * here - 1)

    for r in range(here):
        gram = (members - 1) / inflation * eye
        total = jnp.zeros((members, 1), jnp.float32)
        for b in range(blocks):
            area = area_of(r, b)
            looked = look_ref[b, pl.ds(pos * here + r, 1), :]
            taper = jnp.zeros((1, nobs), jnp.float32)
            for level in range(taper_ref.shape[0]):
                taper = jnp.where(looked == level, taper_ref[level], taper)
            live = jnp.where(lane < live_ref[area], prec_ref[pl.ds(area, 1), :], 0.0)
            values = hxb[slot_of(area)]
            mean = jnp.sum(values, axis=0, keepdims=True) * (1.0 / members)
            pert = values - mean
            weighted = pert * (live * taper)
            innovation = read_ref[pl.ds(area, 1), :] - mean
            gram = gram + mm(weighted, pert, (((1,), (1,)), ((), ())))
            total = total + jnp.sum(weighted * innovation, axis=1, keepdims=True)
        norm = jnp.sqrt(
            jnp.sum(jnp.sum(gram * gram, axis=1, keepdims=True), axis=0, keepdims=True)
        )
        norms.append(norm)
        scaled[r] = gram / norm
        drive[r] = jnp.broadcast_to(total, (members, LANES))

    def correction(r):
        return 1.5 * eye - 0.5 * mm(root[r], scaled[r])

    for r in range(here):
        fix = 1.5 * eye - 0.5 * scaled[r]
        root[r] = fix
        scaled[r] = mm(scaled[r], fix)

    def sweep(step, carry):
        for r in range(here):
            fix = correction(r)
            root[r] = mm(fix, root[r])
            scaled[r] = mm(scaled[r], fix)
        return carry

    lax.fori_loop(1, NSIT - 1, sweep, 0)
    for r in range(here):
        root[r] = mm(correction(r), root[r])
    for r in range(here):
        t = root[r]
        shift = mm(t, mm(t, drive[r])) / norms[r]
        factor = jnp.sqrt(jnp.full((1, 1), members - 1.0, jnp.float32)) / jnp.sqrt(norms[r])
        wide = jnp.concatenate([shift] * (members // LANES), axis=1)
        tb[here + r] = factor * t + wide
    t_pair = beside(tb, t_send, t_recv)
    for copy in t_pair:
        copy.start()
    for copy in t_pair:
        copy.wait()
    for r in range(here):
        shares = [taper_ref[blend_ref[r, 0, b]] for b in range(blocks)]
        whole = shares[0]
        for share in shares[1:]:
            whole = whole + share
        mixed = jnp.zeros((members, members), jnp.float32)
        for b in range(blocks):
            mixed = mixed + shares[b] * tb[slot_of(area_of(r, b))]
        ptt[r] = (mixed / jnp.full((1, 1), whole, jnp.float32)).T

    pair = 2
    own_o = []
    for r in range(here):
        own_x[r].wait()
        for i in range(n - 1):
            x_copy(r, me, partner(i)).wait_recv()
        src = xs.at[r].reshape(members * cols, LANES)
        dst = ob.at[r].reshape(members * cols, LANES)

        def update(step, carry, r=r, src=src, dst=dst):
            first = step * pair
            parts = [src[pl.ds(first + c, members, stride=cols), :] for c in range(pair)]
            values = jnp.concatenate(parts, axis=1)
            center = jnp.sum(values, axis=0, keepdims=True) * (1.0 / members)
            new = center + mm(ptt[r], values - center)
            for c in range(pair):
                dst[pl.ds(first + c, members, stride=cols), :] = new[
                    :, c * LANES : (c + 1) * LANES
                ]
            return carry

        lax.fori_loop(0, cols // pair, update, 0)
        for i in range(n - 1):
            o_copy(r, partner(i), me).start()
        mine = pltpu.make_async_copy(ob.at[r, rows(me)], out_ref.at[r, :, :, me, :], o_local.at[r])
        mine.start()
        own_o.append(mine)
    for copy in own_o:
        copy.wait()
    h_send(me, True, "wait_send", own=True)
    h_send(me, False, "wait_send", own=True)
    for s in range(1, n):
        @pl.when(me - s >= 0)
        def _():
            h_send(me - s, True, "wait_send")

        @pl.when(me + s < n)
        def _():
            h_send(me + s, False, "wait_send")

    for r in range(here):
        for i in range(n - 1):
            x_copy(r, partner(i), me).wait_send()
            o_copy(r, partner(i), me).wait_send()
            o_copy(r, me, partner(i)).wait_recv()


def body(
    n,
    ring,
    prior_states,
    prior_in_sensor_space,
    sensor_readings,
    error_precisions,
    live_tallies,
    adjacent_areas,
    taper_lookup,
    blend_lookup,
    taper_factors,
):
    here, block, tiles, points = prior_states.shape
    members = n * block
    nobs = prior_in_sensor_space.shape[2]
    cols = points // LANES
    assert tiles == n and blend_lookup.shape[1] == 1
    x = prior_states.reshape(here, block, tiles, cols, LANES).transpose(0, 1, 3, 2, 4)
    f32 = jnp.float32
    looks, near = taper_lookup.transpose(1, 0, 2), adjacent_areas.T
    dma = pltpu.SemaphoreType.DMA
    out = pl.pallas_call(
        functools.partial(kernel, n, ring),
        out_shape=jax.ShapeDtypeStruct((here, block, cols, n, LANES), f32),
        in_specs=[pl.BlockSpec(memory_space=pltpu.HBM)] * 9,
        out_specs=pl.BlockSpec(memory_space=pl.ANY),
        scratch_shapes=[
            pltpu.VMEM(sensor_readings.shape, f32),
            pltpu.VMEM(error_precisions.shape, f32),
            pltpu.VMEM(looks.shape, jnp.int32),
            pltpu.SMEM(live_tallies.shape, jnp.int32),
            pltpu.SMEM(near.shape, jnp.int32),
            pltpu.SMEM(blend_lookup.shape, jnp.int32),
            pltpu.SMEM(taper_factors.shape, f32),
            pltpu.VMEM((here, members, cols, LANES), f32),
            pltpu.VMEM((here, members, cols, LANES), f32),
            pltpu.VMEM((3 * here, members, nobs), f32),
            pltpu.VMEM((3 * here, members, members), f32),
            pltpu.VMEM((here, members, members), f32),
            pltpu.VMEM((here, members, members), f32),
            pltpu.VMEM((here, members, LANES), f32),
            pltpu.VMEM((here, members, members), f32),
            dma((here, n)),
            dma((here, n)),
            dma((here,)),
            dma((here, n)),
            dma((here, n)),
            dma((here,)),
            dma((n,)),
            dma((n,)),
            dma((n,)),
            dma,
            dma((7,)),
            dma((2, n)),
            dma((2, n)),
            dma((2,)),
            dma((2,)),
            pltpu.SemaphoreType.REGULAR((5,)),
        ],
        compiler_params=pltpu.CompilerParams(
            collective_id=0, has_side_effects=True, vmem_limit_bytes=48 * 1024 * 1024
        ),
        name="letkf",
    )(
        *[
            pltpu.with_memory_space_constraint(a, pltpu.HBM)
            for a in (
                prior_in_sensor_space,
                sensor_readings,
                error_precisions,
                looks,
                live_tallies,
                near,
                blend_lookup,
                taper_factors,
                x,
            )
        ]
    )
    return out.transpose(0, 1, 3, 2, 4).reshape(here, block, tiles, points)


def solution(mesh):
    n, ring = mesh.shape["member"], mesh.shape["region"]
    placed = (
        P("region", "member", None, None),
        P("region", "member", None),
        P(),
        P(),
        P(),
        P(),
        P(),
        P("region", "member", None),
        P(),
    )
    return jax.shard_map(
        functools.partial(body, n, ring),
        mesh=mesh,
        in_specs=placed,
        out_specs=P("region", "member", None, None),
        check_vma=False,
    )
```

```python
import functools
import jax
import jax.numpy as jnp
from jax import lax
from jax.experimental import pallas as pl
from jax.experimental.pallas import tpu as pltpu
from jax.sharding import PartitionSpec as P

NSIT = 8
LANES = 128
inflation = 1.1
highest = lax.Precision.HIGHEST
MESH = pl.DeviceIdType.MESH


def late_cols(cols):
    return 0, max(3 * cols // 8, 1)


def partner_of(me, n, i):
    up = n - 1 - i
    low = jnp.where(up <= me, up - 1, up)
    return jnp.where(me < n // 2, low, jnp.where(i >= me, i + 1, i))


def by_core(act):
    for core in range(2):
        pl.when(lax.rem(lax.axis_index("region"), 2) == core)(functools.partial(act, core))


def mm(a, b, dims=(((1,), (0,)), ((), ()))):
    return lax.dot_general(a, b, dims, precision=highest, preferred_element_type=jnp.float32)


def kernel(
    n,
    ring,
    hx_ref,
    read_hbm,
    prec_hbm,
    look_hbm,
    live_hbm,
    adj_hbm,
    blend_hbm,
    taper_hbm,
    x_ref,
    out_ref,
    late_ref,
    read_ref,
    prec_ref,
    look_ref,
    live_ref,
    adj_ref,
    blend_ref,
    taper_ref,
    xs,
    ob,
    hxb,
    tb,
    scaled,
    root,
    drive,
    ptt,
    x_send,
    x_recv,
    x_local,
    o_send,
    o_recv,
    o_local,
    late_sem,
    h_up,
    h_down,
    h_recv,
    h_local,
    small,
    n_send,
    n_recv,
    t_send,
    t_recv,
    met,
):
    me = lax.axis_index("member")
    pos = lax.axis_index("region")
    here = x_ref.shape[0]
    block = x_ref.shape[1]
    cols = x_ref.shape[2]
    members = n * block
    nobs = hx_ref.shape[2]
    blocks = look_ref.shape[0]
    left, right = lax.rem(pos + ring - 1, ring), lax.rem(pos + 1, ring)
    half = n // 2
    low = me < half
    inner = jnp.where(low, me + 1, me - 1)
    outer = jnp.where(low, me - 1, me + 1)
    middle = (me == half - 1) | (me == half)
    edge = (me == 0) | (me == n - 1)

    def partner(i):
        return partner_of(me, n, i)

    def far(i):
        up = n - 1 - i
        return jnp.where(low, jnp.where(up < me + 2, up - 2, up), jnp.where(i < me - 1, i, i + 2))

    def tell(sem, **where):
        pl.semaphore_signal(sem, inc=1, device_id=where, device_id_type=MESH)

    barrier = pltpu.get_barrier_semaphore()

    @pl.when(middle)
    def _():
        tell(barrier, member=inner)

    @pl.when(jnp.logical_not(edge))
    def _():
        tell(barrier, member=outer)
        pl.semaphore_wait(barrier, 1)

    @pl.when(edge)
    def _():
        for side in (left, right):
            tell(barrier, region=side)
        pl.semaphore_wait(barrier, 3)

    def rows(who):
        return pl.ds(pl.multiple_of(who * block, block), block)

    def h_copy(owner, up, own=False):
        kept = hxb.at[pl.ds(here, here), rows(owner)]
        return pltpu.make_async_remote_copy(
            hx_ref if own else kept,
            kept,
            (h_up if up else h_down).at[owner],
            h_recv.at[owner],
            device_id={"member": me + 1 if up else me - 1},
            device_id_type=MESH,
        )

    def h_send(owner, up, act, own=False):
        @pl.when(me < n - 1 if up else me > 0)
        def _():
            getattr(h_copy(owner, up, own), act)()

    def x_copy(r, peer, owner):
        return pltpu.make_async_remote_copy(
            x_ref.at[r, :, :, peer, :],
            xs.at[r, rows(owner)],
            x_send.at[r, peer],
            x_recv.at[r, owner],
            device_id={"member": peer},
            device_id_type=MESH,
        )

    def o_copy(r, peer, owner, upto):
        part = pl.ds(0, upto)
        return pltpu.make_async_remote_copy(
            ob.at[r, rows(peer), part],
            out_ref.at[r, :, part, owner, :],
            o_send.at[r, peer],
            o_recv.at[r, owner],
            device_id={"member": peer},
            device_id_type=MESH,
        )

    def o_each(r, act):
        if r < here - 1:
            act(cols)
        else:
            by_core(lambda core: act(cols - late_cols(cols)[core]))

    def beside(buf, send, recv, part=None, src=None):
        def at(slot):
            where = buf.at[pl.ds(slot * here, here)]
            return where if part is None else where.at[:, rows(part)]

        def sems(ref, side):
            return ref.at[side] if part is None else ref.at[side, part]

        mine = at(1) if src is None else src
        return (
            pltpu.make_async_remote_copy(
                mine,
                at(2),
                sems(send, 0),
                sems(recv, 0),
                device_id={"region": left},
                device_id_type=MESH,
            ),
            pltpu.make_async_remote_copy(
                mine,
                at(0),
                sems(send, 1),
                sems(recv, 1),
                device_id={"region": right},
                device_id_type=MESH,
            ),
        )

    def h_beside(owner, src=None):
        return beside(hxb, n_send, n_recv, owner, src)

    own_h = pltpu.make_async_copy(hx_ref, hxb.at[pl.ds(here, here), rows(me)], h_local)
    tables = (
        (read_hbm, read_ref),
        (prec_hbm, prec_ref),
        (look_hbm, look_ref),
        (live_hbm, live_ref),
        (adj_hbm, adj_ref),
        (blend_hbm, blend_ref),
        (taper_hbm, taper_ref),
    )
    fetches = [pltpu.make_async_copy(*t, small.at[i]) for i, t in enumerate(tables)]
    own_x = [
        pltpu.make_async_copy(x_ref.at[r, :, :, me, :], xs.at[r, rows(me)], x_local.at[r])
        for r in range(here)
    ]
    @pl.when(low)
    def _():
        h_copy(me, True, True).start()

    @pl.when(jnp.logical_not(low))
    def _():
        h_copy(me, False, True).start()

    @pl.when(middle)
    def _():
        x_copy(0, inner, me).start()

    @pl.when(jnp.logical_not(edge))
    def _():
        pl.semaphore_wait(met.at[0], 1)

    @pl.when(jnp.logical_not(middle))
    def _():
        tell(met.at[0], member=inner)

    @pl.when(middle)
    def _():
        tell(met.at[1], member=inner)

    pl.semaphore_wait(met.at[1], 1)

    @pl.when(jnp.logical_not(edge))
    def _():
        tell(met.at[1], member=outer)

    @pl.when(low & jnp.logical_not(edge))
    def _():
        h_copy(me, False, True).start()

    @pl.when(jnp.logical_not(low | edge))
    def _():
        h_copy(me, True, True).start()

    @pl.when(jnp.logical_not(middle))
    def _():
        x_copy(0, partner(0), me).start()

    @pl.when(edge)
    def _():
        tell(met.at[2], region=right)
        tell(met.at[3], region=left)
        pl.semaphore_wait(met.at[2], 1)
        pl.semaphore_wait(met.at[3], 1)

        @pl.when(jnp.logical_not(middle))
        def _():
            tell(met.at[4], member=inner)

    for copy in [own_h] + fetches:
        copy.start()

    @pl.when(jnp.logical_not(edge))
    def _():
        pl.semaphore_wait(met.at[4], 1)

        @pl.when(jnp.logical_not(middle))
        def _():
            tell(met.at[4], member=inner)

    for copy in h_beside(me, hx_ref):
        copy.start()
    for s in range(1, n):
        @pl.when(me - s >= 0)
        def _():
            h_copy(me - s, True).wait_recv()
            h_send(me - s, True, "start")
            for copy in h_beside(me - s):
                copy.start()

        @pl.when(me + s < n)
        def _():
            h_copy(me + s, False).wait_recv()
            h_send(me + s, False, "start")
            for copy in h_beside(me + s):
                copy.start()

        if s == 1:
            for i in range(n - 2):
                x_copy(0, jnp.where(middle, far(i), partner(i + 1)), me).start()
    for r in range(1, here):
        for i in range(n - 1):
            x_copy(r, partner(i), me).start()
    for copy in own_x:
        copy.start()
    for copy in [own_h] + fetches:
        copy.wait()
    for owner in range(n):
        for copy in h_beside(owner):
            copy.wait()

    lane = lax.broadcasted_iota(jnp.int32, (1, nobs), 1)
    line = lax.broadcasted_iota(jnp.int32, (members, members), 0)
    cross = lax.broadcasted_iota(jnp.int32, (members, members), 1)
    eye = jnp.where(line == cross, 1.0, 0.0).astype(jnp.float32)
    norms = []

    def area_of(r, b):
        mine = pos * here + r
        return mine if b == 0 else adj_ref[b - 1, mine]

    def slot_of(area):
        slot = lax.rem(area // here - pos + 1 + ring, ring) * here + lax.rem(area, here)
        return jnp.minimum(slot, 3 * here - 1)

    for r in range(here):
        gram = (members - 1) / inflation * eye
        total = jnp.zeros((members, 1), jnp.float32)
        for b in range(blocks):
            area = area_of(r, b)
            looked = look_ref[b, pl.ds(pos * here + r, 1), :]
            taper = jnp.zeros((1, nobs), jnp.float32)
            for level in range(taper_ref.shape[0]):
                taper = jnp.where(looked == level, taper_ref[level], taper)
            live = jnp.where(lane < live_ref[area], prec_ref[pl.ds(area, 1), :], 0.0)
            values = hxb[slot_of(area)]
            mean = jnp.sum(values, axis=0, keepdims=True) * (1.0 / members)
            pert = values - mean
            weighted = pert * (live * taper)
            innovation = read_ref[pl.ds(area, 1), :] - mean
            gram = gram + mm(weighted, pert, (((1,), (1,)), ((), ())))
            total = total + jnp.sum(weighted * innovation, axis=1, keepdims=True)
        norm = jnp.sqrt(
            jnp.sum(jnp.sum(gram * gram, axis=1, keepdims=True), axis=0, keepdims=True)
        )
        norms.append(norm)
        scaled[r] = gram / norm
        drive[r] = jnp.broadcast_to(total, (members, LANES))

    def correction(r):
        return 1.5 * eye - 0.5 * mm(root[r], scaled[r])

    for r in range(here):
        fix = 1.5 * eye - 0.5 * scaled[r]
        root[r] = fix
        scaled[r] = mm(scaled[r], fix)

    def sweep(step, carry):
        for r in range(here):
            fix = correction(r)
            root[r] = mm(fix, root[r])
            scaled[r] = mm(scaled[r], fix)
        return carry

    lax.fori_loop(1, NSIT - 1, sweep, 0)
    for r in range(here):
        root[r] = mm(correction(r), root[r])
    for r in range(here):
        t = root[r]
        shift = mm(t, mm(t, drive[r])) / norms[r]
        factor = jnp.sqrt(jnp.full((1, 1), members - 1.0, jnp.float32)) / jnp.sqrt(norms[r])
        wide = jnp.concatenate([shift] * (members // LANES), axis=1)
        tb[here + r] = factor * t + wide
    t_pair = beside(tb, t_send, t_recv)
    for copy in t_pair:
        copy.start()
    for copy in t_pair:
        copy.wait()
    for r in range(here):
        shares = [taper_ref[blend_ref[r, 0, b]] for b in range(blocks)]
        whole = shares[0]
        for share in shares[1:]:
            whole = whole + share
        mixed = jnp.zeros((members, members), jnp.float32)
        for b in range(blocks):
            mixed = mixed + shares[b] * tb[slot_of(area_of(r, b))]
        ptt[r] = (mixed / jnp.full((1, 1), whole, jnp.float32)).T

    pair = 2
    own_o = []
    for r in range(here):
        own_x[r].wait()
        for i in range(n - 1):
            x_copy(r, me, partner(i)).wait_recv()
        src = xs.at[r].reshape(members * cols, LANES)
        dst = ob.at[r].reshape(members * cols, LANES)

        def update(step, carry, r=r, src=src, dst=dst):
            first = step * pair
            parts = [src[pl.ds(first + c, members, stride=cols), :] for c in range(pair)]
            values = jnp.concatenate(parts, axis=1)
            center = jnp.sum(values, axis=0, keepdims=True) * (1.0 / members)
            new = center + mm(ptt[r], values - center)
            for c in range(pair):
                dst[pl.ds(first + c, members, stride=cols), :] = new[
                    :, c * LANES : (c + 1) * LANES
                ]
            return carry

        lax.fori_loop(0, cols // pair, update, 0)

        def o_start(upto, r=r):
            for i in range(n - 1):
                o_copy(r, partner(i), me, upto).start()

        o_each(r, o_start)
        mine = pltpu.make_async_copy(ob.at[r, rows(me)], out_ref.at[r, :, :, me, :], o_local.at[r])
        mine.start()
        own_o.append(mine)
    wide = late_ref.shape[1]
    late = pltpu.make_async_copy(
        ob.at[here - 1, :, pl.ds(cols - wide, wide)], late_ref, late_sem
    )
    late.start()
    for copy in own_o + [late]:
        copy.wait()
    h_send(me, True, "wait_send", own=True)
    h_send(me, False, "wait_send", own=True)
    for s in range(1, n):
        @pl.when(me - s >= 0)
        def _():
            h_send(me - s, True, "wait_send")

        @pl.when(me + s < n)
        def _():
            h_send(me + s, False, "wait_send")

    for r in range(here):
        for i in range(n - 1):
            x_copy(r, partner(i), me).wait_send()

        def o_wait(upto, r=r):
            for i in range(n - 1):
                o_copy(r, partner(i), me, upto).wait_send()
                o_copy(r, me, partner(i), upto).wait_recv()

        o_each(r, o_wait)


def keep(land_ref, out_ref, sems):
    here, cols = land_ref.shape[0], land_ref.shape[2]

    def move(core):
        copies = []
        for r in range(here):
            upto = cols if r < here - 1 else cols - late_cols(cols)[core]
            part = pl.ds(0, upto)
            copies.append(
                pltpu.make_async_copy(
                    land_ref.at[r, :, part], out_ref.at[r, :, part], sems.at[r]
                )
            )
        for copy in copies:
            copy.start()
        for copy in copies:
            copy.wait()

    by_core(move)


def rest(n, cols, late_ref, kept_ref, out_ref, send, recv, local):
    me = lax.axis_index("member")
    block, wide = out_ref.shape[0], out_ref.shape[1]

    def rows(who):
        return pl.ds(pl.multiple_of(who * block, block), block)

    def move(core):
        some = late_cols(cols)[core]
        if some == 0:
            return
        barrier = pltpu.get_barrier_semaphore()
        for i in range(n - 1):
            pl.semaphore_signal(
                barrier, inc=1, device_id={"member": partner_of(me, n, i)}, device_id_type=MESH
            )
        pl.semaphore_wait(barrier, n - 1)
        part = pl.ds(wide - some, some)

        def copy(peer, owner):
            return pltpu.make_async_remote_copy(
                late_ref.at[rows(peer), part],
                out_ref.at[:, part, owner, :],
                send.at[peer],
                recv.at[owner],
                device_id={"member": peer},
                device_id_type=MESH,
            )

        mine = pltpu.make_async_copy(late_ref.at[rows(me), part], out_ref.at[:, part, me, :], local)
        for i in range(n - 1):
            copy(partner_of(me, n, i), me).start()
        mine.start()
        mine.wait()
        for i in range(n - 1):
            copy(partner_of(me, n, i), me).wait_send()
            copy(me, partner_of(me, n, i)).wait_recv()

    by_core(move)


def join(land_ref, kept_ref, out_ref, sem):
    here, cols, wide = out_ref.shape[0], out_ref.shape[2], land_ref.shape[1]

    def move(core):
        some = late_cols(cols)[core]
        if some == 0:
            return
        copy = pltpu.make_async_copy(
            land_ref.at[:, pl.ds(wide - some, some)],
            out_ref.at[here - 1, :, pl.ds(cols - some, some)],
            sem,
        )
        copy.start()
        copy.wait()

    by_core(move)


def body(
    n,
    ring,
    prior_states,
    prior_in_sensor_space,
    sensor_readings,
    error_precisions,
    live_tallies,
    adjacent_areas,
    taper_lookup,
    blend_lookup,
    taper_factors,
):
    here, block, tiles, points = prior_states.shape
    members = n * block
    nobs = prior_in_sensor_space.shape[2]
    cols = points // LANES
    assert tiles == n and blend_lookup.shape[1] == 1
    x = prior_states.reshape(here, block, tiles, cols, LANES).transpose(0, 1, 3, 2, 4)
    f32 = jnp.float32
    looks, near = taper_lookup.transpose(1, 0, 2), adjacent_areas.T
    dma = pltpu.SemaphoreType.DMA
    whole = jax.ShapeDtypeStruct((here, block, cols, n, LANES), f32)
    wide = max(late_cols(cols))
    hbm = functools.partial(pltpu.with_memory_space_constraint, memory_space=pltpu.HBM)
    in_hbm, anywhere = pl.BlockSpec(memory_space=pltpu.HBM), pl.BlockSpec(memory_space=pl.ANY)
    few = 4 * 1024 * 1024
    land, late = pl.pallas_call(
        functools.partial(kernel, n, ring),
        out_shape=(whole, jax.ShapeDtypeStruct((members, wide, LANES), f32)),
        in_specs=[pl.BlockSpec(memory_space=pltpu.HBM)] * 9,
        out_specs=(anywhere, anywhere),
        scratch_shapes=[
            pltpu.VMEM(sensor_readings.shape, f32),
            pltpu.VMEM(error_precisions.shape, f32),
            pltpu.VMEM(looks.shape, jnp.int32),
            pltpu.SMEM(live_tallies.shape, jnp.int32),
            pltpu.SMEM(near.shape, jnp.int32),
            pltpu.SMEM(blend_lookup.shape, jnp.int32),
            pltpu.SMEM(taper_factors.shape, f32),
            pltpu.VMEM((here, members, cols, LANES), f32),
            pltpu.VMEM((here, members, cols, LANES), f32),
            pltpu.VMEM((3 * here, members, nobs), f32),
            pltpu.VMEM((3 * here, members, members), f32),
            pltpu.VMEM((here, members, members), f32),
            pltpu.VMEM((here, members, members), f32),
            pltpu.VMEM((here, members, LANES), f32),
            pltpu.VMEM((here, members, members), f32),
            dma((here, n)),
            dma((here, n)),
            dma((here,)),
            dma((here, n)),
            dma((here, n)),
            dma((here,)),
            dma,
            dma((n,)),
            dma((n,)),
            dma((n,)),
            dma,
            dma((7,)),
            dma((2, n)),
            dma((2, n)),
            dma((2,)),
            dma((2,)),
            pltpu.SemaphoreType.REGULAR((5,)),
        ],
        compiler_params=pltpu.CompilerParams(
            collective_id=0, has_side_effects=True, vmem_limit_bytes=40 * 1024 * 1024
        ),
        name="letkf",
    )(
        *[
            pltpu.with_memory_space_constraint(a, pltpu.HBM)
            for a in (
                prior_in_sensor_space,
                sensor_readings,
                error_precisions,
                looks,
                live_tallies,
                near,
                blend_lookup,
                taper_factors,
                x,
            )
        ]
    )
    kept = pl.pallas_call(
        keep,
        out_shape=whole,
        in_specs=[anywhere],
        out_specs=in_hbm,
        scratch_shapes=[dma((here,))],
        compiler_params=pltpu.CompilerParams(vmem_limit_bytes=few),
        name="keep",
    )(land)
    kept = hbm(kept)
    last = pl.pallas_call(
        functools.partial(rest, n, cols),
        out_shape=jax.ShapeDtypeStruct((block, wide, n, LANES), f32),
        in_specs=[anywhere, in_hbm],
        out_specs=anywhere,
        scratch_shapes=[dma((n,)), dma((n,)), dma],
        compiler_params=pltpu.CompilerParams(
            collective_id=1, has_side_effects=True, vmem_limit_bytes=few
        ),
        name="rest",
    )(late, kept)
    out = pl.pallas_call(
        join,
        out_shape=whole,
        in_specs=[anywhere, in_hbm],
        out_specs=in_hbm,
        input_output_aliases={1: 0},
        scratch_shapes=[dma],
        compiler_params=pltpu.CompilerParams(vmem_limit_bytes=few),
        name="join",
    )(last, kept)
    return out.transpose(0, 1, 3, 2, 4).reshape(here, block, tiles, points)


def solution(mesh):
    n, ring = mesh.shape["member"], mesh.shape["region"]
    placed = (
        P("region", "member", None, None),
        P("region", "member", None),
        P(),
        P(),
        P(),
        P(),
        P(),
        P("region", "member", None),
        P(),
    )
    return jax.shard_map(
        functools.partial(body, n, ring),
        mesh=mesh,
        in_specs=placed,
        out_specs=P("region", "member", None, None),
        check_vma=False,
    )
```
